32 devices in a mesh: member: 2 (over x), grid: 16 (over z, y, core).
Axes of the slice: x: 2, y: 2, z: 4, core: 2. Of those that a mesh axis runs over, the one named last changes fastest.
Arguments:
- spectrum: bfloat16 [1152, 64, 256], P('grid', 'member'), parts along dimension 1, may hold values from -6 to 6
- ocean_currents: float32 [2, 75, 64, 256], P(None, None, ('member', 'grid')), parts along dimension 2, may hold values from -5 to 5
- wind_stress: float32 [2, 64, 256], P(None, ('member', 'grid')), parts along dimension 1, may hold values from -6 to 6
- land_mask: int32 [32, 256], replicated, may hold values 0 or 1
- bin_drift: float32 [2, 1152], replicated, may hold values from -2 to 2
- coupling_in: bfloat16 [1152, 2048], replicated, may hold values from -0.1875 to 0.1875
- coupling_out: bfloat16 [2048, 1152], replicated, may hold values from -0.125 to 0.125
- stokes_weight: bfloat16 [150, 1152], replicated, may hold values from -0.1875 to 0.1875
- mixing_inverse: float32 [75, 75], replicated, may hold values from -1 to 2
Outputs:
- spectrum_out: bfloat16 [1152, 64, 256], P('grid', 'member'), parts along dimension 1
- currents_out: float32 [2, 75, 64, 256], P(None, None, ('member', 'grid')), parts along dimension 2
The draws below stay inside these ranges and needn't reach their ends.
There are 2 independent parts, one for each index of `member`. The reference program is written for one: setup_inputs(seed, part) draws one part's arguments, and reference() takes and returns one part's arrays. A program takes and returns all parts, laid end to end along the dimension named above; an argument that names none is the same for every part. Nothing has to cross between parts.
All inputs are finite; a program needn't handle non-finite values.
Results may differ from the reference program's by a relative error of at most 0.0061.
Values may be sent and summed in bfloat16 or wider, within the bound.
No kernel may reach another device: no remote copies, remote signals or barrier semaphores. Data moves between devices by JAX's collectives and lax.ppermute only.
A program may use at most 64 MiB of HBM per device.

```python
import math
import jax
import jax.numpy as jnp
from jax import lax

NB = 1152
NINT = 2048
NLEV = 75
NCOL = 256
STEPS = 2
NROW = 32


def draw_mixing_inverse(key, part):
    noise = jnp.clip(jax.random.normal(key, (NLEV, NLEV), jnp.float32), -4.0, 4.0) * (0.45 / math.sqrt(NLEV))
    return 0.6 * jnp.eye(NLEV, dtype=jnp.float32) + noise


def plant(entries, rng, low, high):
    index_at = [jax.random.randint(jax.random.fold_in(rng, axis), (), 0, length) for axis, length in enumerate(entries.shape)]
    widest = entries.shape.index(max(entries.shape))
    beside = index_at[:widest] + [(index_at[widest] + 1) % entries.shape[widest]] + index_at[widest + 1:]
    return entries.at[tuple(index_at)].set(low).at[tuple(beside)].set(high)


def steps_of(own_key, shape, pieces, low, top_value):
    def one(position, blocks):
        steps = jax.random.uniform(jax.random.fold_in(jax.random.fold_in(own_key, 6), position), (blocks,), jnp.float32, low / len(pieces), top_value / len(pieces))
        return jnp.repeat(jnp.exp(steps), shape[position] // blocks).reshape((-1,) + (1,) * (len(shape) - position - 1))

    loudness = one(*pieces[0])
    for cut in pieces[1:]:
        loudness = loudness * one(*cut)
    return loudness


def scatter_about(own_key, extent, deviation, limit, shards=(), kind=jnp.bfloat16):
    drawn = deviation * jax.random.normal(own_key, extent, jnp.float32)
    if shards:
        drawn = drawn * steps_of(own_key, extent, shards, -0.22, 0.18)
    return jnp.clip(drawn, -limit, limit).astype(kind)


def setup_inputs(seed: int = 0, part: int = 0) -> dict:
    splits = jax.random.split(jax.random.key(seed), 10)
    part_keys = jax.random.split(jax.random.fold_in(splits[9], part), 10)
    return {
        "spectrum": scatter_about(part_keys[0], (NB, NROW, NCOL), 1.0, 6.0, ((0, 16),)),
        "ocean_currents": scatter_about(part_keys[1], (2, NLEV, NROW, NCOL), 0.7, 5.0, ((2, 16),), jnp.float32),
        "wind_stress": scatter_about(part_keys[2], (2, NROW, NCOL), 1.0, 6.0, ((1, 16),), jnp.float32),
        "land_mask": plant((jax.random.randint(splits[3], (NROW, NCOL), 0, 4) < 3).astype(jnp.int32), jax.random.fold_in(splits[3], 1), 0, 1),
        "bin_drift": jnp.clip(jax.random.uniform(splits[4], (2, NB), jnp.float32, -2.0, 2.0), -2.0, 2.0),
        "coupling_in": scatter_about(splits[5], (NB, NINT), NB ** -0.5, 0.1875),
        "coupling_out": scatter_about(splits[6], (NINT, NB), NINT ** -0.5, 0.125),
        "stokes_weight": scatter_about(splits[7], (2 * NLEV, NB), NB ** -0.5, 0.1875),
        "mixing_inverse": draw_mixing_inverse(jax.random.fold_in(splits[9], 71), part),
    }


time_step = 0.4
diffusion = 0.15
reach = 0.45


def advect(center, above, below, east_flow, north_flow, drift, land):
    speed_x = reach * jnp.tanh(drift[0][:, None, None] + east_flow[None])
    speed_y = reach * jnp.tanh(drift[1][:, None, None] + north_flow[None])
    western = jnp.roll(center, 1, axis=2)
    eastern = jnp.roll(center, -1, axis=2)
    change = jnp.maximum(speed_x, 0.0) * (center - western) + jnp.minimum(speed_x, 0.0) * (eastern - center)
    change = change + jnp.maximum(speed_y, 0.0) * (center - above) + jnp.minimum(speed_y, 0.0) * (below - center)
    return (center - change) * land[None]


def interact(points, coupling_in, coupling_out, stokes_weight):
    bins, rows, cols = points.shape
    flat = points.reshape(bins, rows * cols)
    terms = lax.dot_general(flat, coupling_in, (((0,), (0,)), ((), ())), preferred_element_type=jnp.float32)
    active = (terms * jnp.tanh(terms)).astype(jnp.bfloat16)
    source = lax.dot_general(coupling_out, active, (((0,), (1,)), ((), ())), preferred_element_type=jnp.float32)
    updated = (flat.astype(jnp.float32) + source).astype(jnp.bfloat16)
    profile = jnp.dot(stokes_weight, updated, preferred_element_type=jnp.float32)
    return updated.reshape(bins, rows, cols), profile.reshape(2, -1, rows, cols)


def ocean_update(padded, stokes, wind, inverse, land, latitude):
    center = padded[:, :, 1:-1]
    lateral = diffusion * (padded[:, :, :-2] + padded[:, :, 2:] + jnp.roll(center, 1, axis=3) + jnp.roll(center, -1, axis=3) - 4.0 * center)
    coriolis = latitude[None, :, None]
    eastward = center[0] + time_step * coriolis * (center[1] + stokes[1]) + lateral[0]
    northward = center[1] - time_step * coriolis * (center[0] + stokes[0]) + lateral[1]
    eastward = eastward.at[0].add(time_step * wind[0])
    northward = northward.at[0].add(time_step * wind[1])
    forced = jnp.stack([eastward, northward])
    mixed = jnp.einsum('kl,slrc->skrc', inverse, forced, precision=lax.Precision.HIGHEST)
    return mixed * land[None, None]


def pad_rows(field, axis):
    shape = list(field.shape)
    shape[axis] = 1
    zero_rows = jnp.zeros(shape, field.dtype)
    return jnp.concatenate([zero_rows, field, zero_rows], axis=axis)


def reference(spectrum, ocean_currents, wind_stress, land_mask, bin_drift, coupling_in, coupling_out, stokes_weight, mixing_inverse):
    land = land_mask.astype(jnp.float32)
    row_place = jnp.arange(NROW).astype(jnp.float32)
    latitude = jnp.sin(math.pi * ((row_place + 0.5) / NROW - 0.5))
    spectra = spectrum
    ocean = ocean_currents
    for turn_index in range(STEPS):
        padded = pad_rows(spectra.astype(jnp.float32), 1)
        moved = advect(padded[:, 1:-1], padded[:, :-2], padded[:, 2:], ocean[0, 0], ocean[1, 0], bin_drift, land).astype(jnp.bfloat16)
        spectra, stokes = interact(moved, coupling_in, coupling_out, stokes_weight)
        ocean = ocean_update(pad_rows(ocean, 2), stokes, wind_stress, mixing_inverse, land, latitude)
    return spectra, ocean
```

```python
import functools
import math

import jax
import jax.numpy as jnp
from jax import lax
from jax.experimental import pallas as pl
from jax.experimental.pallas import tpu as pltpu
from jax.sharding import PartitionSpec as P

STEPS = 2

time_step = 0.4
diffusion = 0.15
reach = 0.45
VMEM = pl.BlockSpec(memory_space=pltpu.VMEM)
LIMIT = 60 * 1024 * 1024


def upwind(f, above, below, drift_x, drift_y, east, north, land):
    cols = f.shape[1]
    speed_x = reach * jnp.tanh(drift_x + east)
    speed_y = reach * jnp.tanh(drift_y + north)
    west = f - pltpu.roll(f, 1, 1)
    step_x = jnp.where(speed_x > 0.0, west, pltpu.roll(west, cols - 1, 1))
    step_y = jnp.where(speed_y > 0.0, f - above, below - f)
    return (f - (speed_x * step_x + speed_y * step_y)) * land


def wide(ref, axis, rows, cols):
    part = ref[axis, rows, :]
    return jnp.concatenate([part] * (cols // part.shape[1]), axis=1)


def move_bins_kernel(me_ref, spec_ref, ocean_ref, land_ref, drift_ref, out_ref, *planes):
    bins, rows, cols = spec_ref.shape
    devices, _, row_dev, _ = ocean_ref.shape
    first = pl.multiple_of(me_ref[0] * bins, 8)

    @pl.loop(0, bins)
    def _(b):
        plane = spec_ref[b].astype(jnp.float32)
        for h, ref in enumerate(planes):
            ref[pl.ds(b * rows, rows), :] = plane[:, h * 128 : (h + 1) * 128]

    size = 24 if bins % 24 == 0 else 8

    def row(b, r):
        return jnp.concatenate(
            [ref[pl.ds(b * rows + r, size, stride=rows), :] for ref in planes], axis=1
        )

    @pl.loop(0, devices)
    def _(d):
        for j in range(row_dev):
            r = d * row_dev + j
            land = land_ref[pl.ds(r, 1), :].astype(jnp.float32)
            east, north = (ocean_ref[d, s, j : j + 1, :] for s in range(2))
            for b in range(0, bins, size):
                f = row(b, r)
                above = row(b, jnp.maximum(r - 1, 0))
                below = row(b, jnp.minimum(r + 1, rows - 1))
                above = jnp.where(r > 0, above, 0.0)
                below = jnp.where(r < rows - 1, below, 0.0)
                here = pl.ds(pl.multiple_of(first + b, 8), size)
                moved = upwind(
                    f, above, below, wide(drift_ref, 0, here, cols), wide(drift_ref, 1, here, cols), east, north, land
                )
                out_ref[d, b : b + size, j * cols : (j + 1) * cols] = moved.astype(jnp.bfloat16)


def move_bins(me, spectrum, ocean_top, land_mask, drift):
    bins, rows, cols = spectrum.shape
    devices, _, row_dev, _ = ocean_top.shape
    return pl.pallas_call(
        move_bins_kernel,
        out_shape=jax.ShapeDtypeStruct((devices, bins, row_dev * cols), jnp.bfloat16),
        in_specs=[pl.BlockSpec(memory_space=pltpu.SMEM)] + [VMEM] * 4,
        out_specs=VMEM,
        scratch_shapes=[pltpu.VMEM((bins * rows, 128), jnp.float32)] * (cols // 128),
        compiler_params=pltpu.CompilerParams(vmem_limit_bytes=20 * 1024 * 1024),
        cost_estimate=pl.CostEstimate(flops=40 * spectrum.size, bytes_accessed=4 * spectrum.size, transcendentals=2 * spectrum.size),
        name="move_bins",
    )(me, spectrum, ocean_top, land_mask, drift)


def tile_of(total, most):
    return next(t for t in range(most - most % 8, 0, -8) if total % t == 0)


def interact_body(moved_ref, win_ref, wout_ref, stokes_ref, active, updated_refs, whole, profile_ref, tk, tm):
    terms_count, bins = win_ref.shape

    @pl.loop(0, terms_count // tk)
    def _(i):
        at = pl.ds(pl.multiple_of(i * tk, tk), tk)
        terms = jnp.dot(win_ref[at, :], moved_ref[...], preferred_element_type=jnp.float32)
        active[at, :] = (terms * jnp.tanh(terms)).astype(jnp.bfloat16)

    @pl.loop(0, bins // tm)
    def _(i):
        at = pl.ds(pl.multiple_of(i * tm, 8), tm)
        source = jnp.dot(wout_ref[at, :], active[...], preferred_element_type=jnp.float32)
        updated = (moved_ref[at, :].astype(jnp.float32) + source).astype(jnp.bfloat16)
        whole[at, :] = updated
        width = updated.shape[1] // max(1, len(updated_refs))
        for j, ref in enumerate(updated_refs):
            ref[at, :] = updated[:, j * width : (j + 1) * width]

    for s in range(2):
        profile_ref[s] = jnp.dot(stokes_ref[s], whole[...], preferred_element_type=jnp.float32)


def first_kernel(moved_ref, win_ref, wout_ref, stokes_ref, *refs):
    *updated_refs, profile_ref, active, whole = refs
    tk, tm = tile_of(win_ref.shape[0], 1024), tile_of(wout_ref.shape[0], 576)
    interact_body(moved_ref, win_ref, wout_ref, stokes_ref, active, updated_refs, whole, profile_ref, tk, tm)


def first_step(moved, win, wout, stokes, row_dev):
    bins, points = moved.shape
    terms, levels = win.shape[0], stokes.shape[1]
    return pl.pallas_call(
        first_kernel,
        out_shape=[jax.ShapeDtypeStruct((bins, points // row_dev), jnp.bfloat16)] * row_dev
        + [jax.ShapeDtypeStruct((2, levels, points), jnp.float32)],
        in_specs=[VMEM] * 4,
        out_specs=[VMEM] * (row_dev + 1),
        scratch_shapes=[pltpu.VMEM((terms, points), jnp.bfloat16), pltpu.VMEM((bins, points), jnp.bfloat16)],
        compiler_params=pltpu.CompilerParams(vmem_limit_bytes=24 * 1024 * 1024),
        cost_estimate=pl.CostEstimate(flops=4 * bins * terms * points, bytes_accessed=4 * bins * terms, transcendentals=terms * points),
        name="first_step",
    )(moved, win, wout, stokes)


def second_kernel(win_ref, wout_ref, stokes_ref, drift_ref, ocean_ref, land_ref, *refs):
    *row_refs, whole, profile_ref, active, moved = refs
    bins, cols = row_refs[0].shape
    row_dev = len(row_refs) - 2
    size = 16

    @pl.loop(0, bins // size)
    def _(i):
        at = pl.ds(pl.multiple_of(i * size, size), size)
        rows = [ref[at, :].astype(jnp.float32) for ref in row_refs]
        drift_x, drift_y = (wide(drift_ref, s, at, cols) for s in range(2))
        for j in range(row_dev):
            lanes = slice(j * cols, (j + 1) * cols)
            east, north = (ocean_ref[s, 0:1, lanes] for s in range(2))
            new = upwind(rows[j + 1], rows[j], rows[j + 2], drift_x, drift_y, east, north, land_ref[:, lanes])
            moved[at, lanes] = new.astype(jnp.bfloat16)

    tk, tm = tile_of(win_ref.shape[0], 1024), tile_of(wout_ref.shape[0], 576)
    interact_body(moved, win_ref, wout_ref, stokes_ref, active, (), whole, profile_ref, tk, tm)


def second_step(rows, win, wout, stokes, drift, ocean, land):
    bins, cols = rows[0].shape
    points = cols * (len(rows) - 2)
    terms, levels = win.shape[0], stokes.shape[1]
    return pl.pallas_call(
        second_kernel,
        out_shape=[
            jax.ShapeDtypeStruct((bins, points), jnp.bfloat16),
            jax.ShapeDtypeStruct((2, levels, points), jnp.float32),
        ],
        in_specs=[VMEM] * (6 + len(rows)),
        out_specs=[VMEM] * 2,
        scratch_shapes=[pltpu.VMEM((terms, points), jnp.bfloat16), pltpu.VMEM((bins, points), jnp.bfloat16)],
        compiler_params=pltpu.CompilerParams(vmem_limit_bytes=24 * 1024 * 1024),
        cost_estimate=pl.CostEstimate(flops=4 * bins * terms * points, bytes_accessed=4 * bins * terms, transcendentals=terms * points),
        name="second_step",
    )(win, wout, stokes, drift, ocean, land, *rows)


def ocean_kernel(ocean_ref, above_ref, below_ref, profile_ref, wind_ref, inverse_ref, land_ref, latitude_ref, out_ref):
    levels, points = ocean_ref.shape[1:]
    cols = above_ref.shape[2]
    row_dev = points // cols
    turn = time_step * latitude_ref[...]
    top = lax.broadcasted_iota(jnp.int32, (levels, points), 0) == 0
    for s in range(2):
        center = ocean_ref[s]
        other = ocean_ref[1 - s] + profile_ref[1 - s]
        pieces = [center[:, j * cols : (j + 1) * cols] for j in range(row_dev)]
        rows = [above_ref[s]] + pieces + [below_ref[s]]
        around = [
            rows[j] + rows[j + 2] + pltpu.roll(rows[j + 1], 1, 1) + pltpu.roll(rows[j + 1], cols - 1, 1)
            for j in range(row_dev)
        ]
        lateral = diffusion * (jnp.concatenate(around, axis=1) - 4.0 * center)
        swing = turn * other
        forced = center + (swing if s == 0 else -swing) + lateral
        forced = forced + jnp.where(top, time_step * wind_ref[s : s + 1, :], 0.0)
        mixed = jnp.dot(inverse_ref[...], forced, precision=lax.Precision.HIGHEST, preferred_element_type=jnp.float32)
        out_ref[s] = mixed * land_ref[...]


def ocean_step(ocean, above, below, profile, wind, inverse, land, latitude):
    return pl.pallas_call(
        ocean_kernel,
        out_shape=jax.ShapeDtypeStruct(ocean.shape, jnp.float32),
        in_specs=[VMEM] * 8,
        out_specs=VMEM,
        compiler_params=pltpu.CompilerParams(vmem_limit_bytes=8 * 1024 * 1024),
        cost_estimate=pl.CostEstimate(flops=12 * inverse.shape[0] * ocean.size, bytes_accessed=12 * ocean.size, transcendentals=0),
        name="ocean_step",
    )(ocean, above, below, profile, wind, inverse, land, latitude)


def gather_kernel(parts_ref, out_ref, *planes):
    devices, bins, points = parts_ref.shape
    rows, cols = out_ref.shape[1:]
    row_dev = rows // devices
    size = 24 if bins % 24 == 0 else 8

    @pl.loop(0, devices)
    def _(d):
        for b in range(0, bins, size):
            part = parts_ref[d, b : b + size, :].astype(jnp.float32)
            for j in range(row_dev):
                at = pl.ds(b * rows + d * row_dev + j, size, stride=rows)
                for h, ref in enumerate(planes):
                    low = j * cols + h * 128
                    ref[at, :] = part[:, low : low + 128]

    @pl.loop(0, bins)
    def _(b):
        plane = [ref[pl.ds(b * rows, rows), :] for ref in planes]
        out_ref[b] = jnp.concatenate(plane, axis=1).astype(jnp.bfloat16)


def gather_rows(parts, rows, cols):
    bins = parts.shape[1]
    return pl.pallas_call(
        gather_kernel,
        out_shape=jax.ShapeDtypeStruct((bins, rows, cols), jnp.bfloat16),
        in_specs=[VMEM],
        out_specs=VMEM,
        scratch_shapes=[pltpu.VMEM((bins * rows, 128), jnp.float32)] * (cols // 128),
        compiler_params=pltpu.CompilerParams(vmem_limit_bytes=20 * 1024 * 1024),
        cost_estimate=pl.CostEstimate(flops=parts.size, bytes_accessed=4 * parts.size, transcendentals=0),
        name="gather_rows",
    )(parts)


def shifts(size):
    up = [(i, i + 1) for i in range(size - 1)]
    return up, [(j, i) for i, j in up]


def exchange(value):
    return lax.all_to_all(value, "grid", split_axis=0, concat_axis=0, tiled=True)


def per_device(
    spectrum,
    ocean_currents,
    wind_stress,
    land_mask,
    bin_drift,
    coupling_in,
    coupling_out,
    stokes_weight,
    mixing_inverse,
):
    device = lax.axis_index("grid")
    devices = lax.axis_size("grid")
    bins, rows, cols = spectrum.shape
    row_dev = rows // devices
    levels = ocean_currents.shape[1]
    points = row_dev * cols
    up, down = shifts(devices)
    me = device.astype(jnp.int32).reshape(1)

    tops = jnp.broadcast_to(ocean_currents[:, 0][None], (devices, 2, row_dev, cols))
    tops = exchange(tops)
    ocean_above = lax.ppermute(ocean_currents[:, :, -1], "grid", up)
    ocean_below = lax.ppermute(ocean_currents[:, :, 0], "grid", down)

    win = coupling_in.T
    wout = coupling_out.T
    stokes = stokes_weight.reshape(2, levels, -1)
    drift = jnp.broadcast_to(bin_drift[:, :, None], bin_drift.shape + (128,))
    land = lax.dynamic_slice_in_dim(land_mask, device * row_dev, row_dev, 0)
    land = land.astype(jnp.float32).reshape(1, points)
    place = (device * row_dev + jnp.arange(row_dev, dtype=jnp.int32)).astype(jnp.float32)
    latitude = jnp.sin(math.pi * ((place + 0.5) / rows - 0.5))
    latitude = jnp.broadcast_to(latitude[:, None], (row_dev, cols)).reshape(1, points)
    wind = wind_stress.reshape(2, points)
    ocean = ocean_currents.reshape(2, levels, points)

    moved = exchange(move_bins(me, spectrum, tops, land_mask, drift))
    *updated, profile = first_step(moved.reshape(-1, points), win, wout, stokes, row_dev)
    above = lax.ppermute(updated[-1], "grid", up)
    below = lax.ppermute(updated[0], "grid", down)
    ocean = ocean_step(ocean, ocean_above, ocean_below, profile, wind, mixing_inverse, land, latitude)
    whole, profile = second_step([above, *updated, below], win, wout, stokes, drift, ocean, land)
    spectra = exchange(whole.reshape(devices, bins, points))
    ocean_above = lax.ppermute(ocean[:, :, -cols:], "grid", up)
    ocean_below = lax.ppermute(ocean[:, :, :cols], "grid", down)
    ocean = ocean_step(ocean, ocean_above, ocean_below, profile, wind, mixing_inverse, land, latitude)
    return gather_rows(spectra, rows, cols), ocean.reshape(2, levels, row_dev, cols)


def padded_2(value, sides, width):
    for axis, dim in sides:
        size, length = (lax.axis_size(axis), value.shape[dim])
        up = [(i, (i + 1) % size) for i in range(size - 1)]
        down = [(j, i) for i, j in up]
        last = lax.slice_in_dim(value, length - width, length, axis=dim)
        first = lax.slice_in_dim(value, 0, width, axis=dim)
        before = lax.ppermute(last, axis, up)
        after = lax.ppermute(first, axis, down)
        value = jnp.concatenate([before, value, after], axis=dim)
    return value


def plain_advect(center, above, below, east_flow, north_flow, drift, land):
    speed_x = reach * jnp.tanh(drift[0][:, None, None] + east_flow[None])
    speed_y = reach * jnp.tanh(drift[1][:, None, None] + north_flow[None])
    western = jnp.roll(center, 1, axis=2)
    eastern = jnp.roll(center, -1, axis=2)
    change = jnp.maximum(speed_x, 0.0) * (center - western) + jnp.minimum(speed_x, 0.0) * (
        eastern - center
    )
    change = (
        change
        + jnp.maximum(speed_y, 0.0) * (center - above)
        + jnp.minimum(speed_y, 0.0) * (below - center)
    )
    return (center - change) * land[None]


def plain_interact(points, coupling_in, coupling_out, stokes_weight):
    bins, rows, cols = points.shape
    flat = points.reshape(bins, rows * cols)
    terms = lax.dot_general(
        flat, coupling_in, (((0,), (0,)), ((), ())), preferred_element_type=jnp.float32
    )
    active = (terms * jnp.tanh(terms)).astype(jnp.bfloat16)
    source = lax.dot_general(
        coupling_out, active, (((0,), (1,)), ((), ())), preferred_element_type=jnp.float32
    )
    updated = (flat.astype(jnp.float32) + source).astype(jnp.bfloat16)
    profile = jnp.dot(stokes_weight, updated, preferred_element_type=jnp.float32)
    return (updated.reshape(bins, rows, cols), profile.reshape(2, -1, rows, cols))


def plain_ocean_update(padded, stokes, wind, inverse, land, latitude):
    center = padded[:, :, 1:-1]
    lateral = diffusion * (
        padded[:, :, :-2]
        + padded[:, :, 2:]
        + jnp.roll(center, 1, axis=3)
        + jnp.roll(center, -1, axis=3)
        - 4.0 * center
    )
    coriolis = latitude[None, :, None]
    eastward = center[0] + time_step * coriolis * (center[1] + stokes[1]) + lateral[0]
    northward = center[1] - time_step * coriolis * (center[0] + stokes[0]) + lateral[1]
    eastward = eastward.at[0].add(time_step * wind[0])
    northward = northward.at[0].add(time_step * wind[1])
    forced = jnp.stack([eastward, northward])
    mixed = jnp.einsum("kl,slrc->skrc", inverse, forced, precision=lax.Precision.HIGHEST)
    return mixed * land[None, None]


def plain_device(
    spectrum,
    ocean_currents,
    wind_stress,
    land_mask,
    bin_drift,
    coupling_in,
    coupling_out,
    stokes_weight,
    mixing_inverse,
):
    device = lax.axis_index("grid")
    device_count = lax.axis_size("grid")
    rows_dev = ocean_currents.shape[2]
    total_rows = rows_dev * device_count
    land = land_mask.astype(jnp.float32)
    land_local = lax.dynamic_slice_in_dim(land, device * rows_dev, rows_dev, 0)
    row_place = (device * rows_dev + jnp.arange(rows_dev, dtype=jnp.int32)).astype(jnp.float32)
    latitude = jnp.sin(math.pi * ((row_place + 0.5) / total_rows - 0.5))
    ocean = ocean_currents
    points = lax.all_to_all(spectrum, "grid", split_axis=1, concat_axis=0, tiled=True)
    for turn_index in range(STEPS):
        padded = padded_2(points, (("grid", 1),), 1).astype(jnp.float32)
        moved = plain_advect(
            padded[:, 1:-1],
            padded[:, :-2],
            padded[:, 2:],
            ocean[0, 0],
            ocean[1, 0],
            bin_drift,
            land_local,
        ).astype(jnp.bfloat16)
        updated, stokes = plain_interact(moved, coupling_in, coupling_out, stokes_weight)
        ocean_padded = padded_2(ocean, (("grid", 2),), 1)
        points = updated
        ocean = plain_ocean_update(
            ocean_padded, stokes, wind_stress, mixing_inverse, land_local, latitude
        )
    spectra = lax.all_to_all(points, "grid", split_axis=0, concat_axis=1, tiled=True)
    return (spectra, ocean)


def solution(mesh):
    def body(spectrum, *others):
        aligned = spectrum.shape[0] % 8 == 0 and spectrum.shape[2] % 128 == 0
        return (per_device if aligned else plain_device)(spectrum, *others)

    return jax.shard_map(
        body,
        mesh=mesh,
        in_specs=(
            P("grid", "member", None),
            P(None, None, ("member", "grid"), None),
            P(None, ("member", "grid"), None),
            P(),
            P(),
            P(),
            P(),
            P(),
            P(),
        ),
        out_specs=(P("grid", "member", None), P(None, None, ("member", "grid"), None)),
        check_vma=False,
    )
```

```python
import functools
import math

import jax
import jax.numpy as jnp
from jax import lax
from jax.experimental import pallas as pl
from jax.experimental.pallas import tpu as pltpu
from jax.sharding import PartitionSpec as P

STEPS = 2

time_step = 0.4
diffusion = 0.15
reach = 0.45
VMEM = pl.BlockSpec(memory_space=pltpu.VMEM)
LIMIT = 60 * 1024 * 1024


def upwind(f, above, below, drift_x, drift_y, east, north, land):
    cols = f.shape[1]
    speed_x = reach * jnp.tanh(drift_x + east)
    speed_y = reach * jnp.tanh(drift_y + north)
    west = f - pltpu.roll(f, 1, 1)
    step_x = jnp.where(speed_x > 0.0, west, pltpu.roll(west, cols - 1, 1))
    step_y = jnp.where(speed_y > 0.0, f - above, below - f)
    return (f - (speed_x * step_x + speed_y * step_y)) * land


def wide(ref, axis, rows, cols):
    part = ref[axis, rows, :]
    return jnp.concatenate([part] * (cols // part.shape[1]), axis=1)


PAD = 8


def move_bins_kernel(me_ref, spec_ref, ocean_ref, land_ref, drift_ref, out_ref, *planes):
    bins, rows, cols = spec_ref.shape
    devices, _, row_dev, _ = ocean_ref.shape
    pitch = rows + PAD
    first = pl.multiple_of(me_ref[0] * bins, 8)

    @pl.loop(0, bins, unroll=8)
    def _(b):
        plane = spec_ref[b].astype(jnp.float32)
        for h, ref in enumerate(planes):
            ref[pl.ds(pl.multiple_of(b * pitch, 8), rows), :] = plane[:, h * 128 : (h + 1) * 128]

    size = 24 if bins % 24 == 0 else 8

    def row(b, r):
        at = pl.ds(b * pitch + r, size, stride=pitch)
        return jnp.concatenate([ref[at, :] for ref in planes], axis=1)

    @pl.loop(0, devices, unroll=2)
    def _(d):
        low = d * row_dev
        for b in range(0, bins, size):
            here = pl.ds(pl.multiple_of(first + b, 8), size)
            drift_x, drift_y = (wide(drift_ref, s, here, cols) for s in range(2))
            field = [row(b, jnp.maximum(low - 1, 0))]
            field += [row(b, low + j) for j in range(row_dev)]
            field += [row(b, jnp.minimum(low + row_dev, rows - 1))]
            field[0] = jnp.where(d > 0, field[0], 0.0)
            field[-1] = jnp.where(d < devices - 1, field[-1], 0.0)
            for j in range(row_dev):
                land = land_ref[pl.ds(low + j, 1), :].astype(jnp.float32)
                east, north = (ocean_ref[d, s, j : j + 1, :] for s in range(2))
                moved = upwind(field[j + 1], field[j], field[j + 2], drift_x, drift_y, east, north, land)
                out_ref[d, b : b + size, j * cols : (j + 1) * cols] = moved.astype(jnp.bfloat16)


def move_bins(me, spectrum, ocean_top, land_mask, drift):
    bins, rows, cols = spectrum.shape
    devices, _, row_dev, _ = ocean_top.shape
    return pl.pallas_call(
        move_bins_kernel,
        out_shape=jax.ShapeDtypeStruct((devices, bins, row_dev * cols), jnp.bfloat16),
        in_specs=[pl.BlockSpec(memory_space=pltpu.SMEM)] + [VMEM] * 4,
        out_specs=VMEM,
        scratch_shapes=[pltpu.VMEM((bins * (rows + PAD), 128), jnp.float32)] * (cols // 128),
        compiler_params=pltpu.CompilerParams(vmem_limit_bytes=20 * 1024 * 1024),
        cost_estimate=pl.CostEstimate(flops=40 * spectrum.size, bytes_accessed=4 * spectrum.size, transcendentals=2 * spectrum.size),
        name="move_bins",
    )(me, spectrum, ocean_top, land_mask, drift)


def turn_kernel(step, win_ref, wout_ref, win_t, wout_t, win_buf, wout_buf, sems):
    jobs = []
    for n, (source, target, buf) in enumerate(((win_ref, win_t, win_buf), (wout_ref, wout_t, wout_buf))):
        for i in range(source.shape[1] // step):
            lanes = slice(i * step, (i + 1) * step)
            copy = pltpu.make_async_copy(source.at[:, lanes], buf.at[i % 2], sems.at[n, i % 2])
            jobs.append((copy, target, lanes, buf, i % 2))
    jobs[0][0].start()
    for k, (copy, target, lanes, buf, slot) in enumerate(jobs):
        if k + 1 < len(jobs):
            jobs[k + 1][0].start()
        copy.wait()
        target[lanes, :] = buf[slot].T


def turn_weights(coupling_in, coupling_out):
    step = 128
    return pl.pallas_call(
        functools.partial(turn_kernel, step),
        out_shape=[jax.ShapeDtypeStruct(w.shape[::-1], w.dtype) for w in (coupling_in, coupling_out)],
        in_specs=[pl.BlockSpec(memory_space=pl.ANY)] * 2,
        out_specs=[VMEM] * 2,
        scratch_shapes=[pltpu.VMEM((2, w.shape[0], step), w.dtype) for w in (coupling_in, coupling_out)]
        + [pltpu.SemaphoreType.DMA((2, 2))],
        compiler_params=pltpu.CompilerParams(vmem_limit_bytes=8 * 1024 * 1024),
        cost_estimate=pl.CostEstimate(flops=0, bytes_accessed=8 * coupling_in.size, transcendentals=0),
        name="turn_weights",
    )(coupling_in, coupling_out)


def tile_of(total, most):
    return next(t for t in range(most - most % 8, 0, -8) if total % t == 0)


def weight_copies(refs, buffers, sems):
    copies = []
    for n, (ref, buffer) in enumerate(zip(refs, buffers)):
        tile = ref.shape[0] // sems.shape[1]
        rows = [pl.ds(i * tile, tile) for i in range(sems.shape[1])]
        copies.append([(at, pltpu.make_async_copy(ref.at[at, :], buffer.at[at, :], sems.at[n, i])) for i, at in enumerate(rows)])
    for group in copies:
        for _, copy in group:
            copy.start()
    return copies


def interact_body(copies, buffers, moved_ref, active, updated_refs):
    win, wout = buffers
    for at, copy in copies[0]:
        copy.wait()
        terms = jnp.dot(win[at, :], moved_ref[...], preferred_element_type=jnp.float32)
        active[at, :] = (terms * jnp.tanh(terms)).astype(jnp.bfloat16)
    for at, copy in copies[1]:
        copy.wait()
        source = jnp.dot(wout[at, :], active[...], preferred_element_type=jnp.float32)
        updated = (moved_ref[at, :].astype(jnp.float32) + source).astype(jnp.bfloat16)
        width = updated.shape[1] // len(updated_refs)
        for j, ref in enumerate(updated_refs):
            ref[at, :] = updated[:, j * width : (j + 1) * width]


def weight_scratch(win, wout, points):
    pieces = 4
    return [
        pltpu.VMEM(win.shape, win.dtype),
        pltpu.VMEM(wout.shape, wout.dtype),
        pltpu.VMEM((win.shape[0], points), jnp.bfloat16),
        pltpu.SemaphoreType.DMA((2, pieces)),
    ]


ANY = pl.BlockSpec(memory_space=pl.ANY)


def in_hbm(*arrays):
    return [pltpu.with_memory_space_constraint(x, pltpu.HBM) for x in arrays]


def first_kernel(moved_ref, win_ref, wout_ref, *refs):
    *updated_refs, win, wout, active, sems = refs
    copies = weight_copies((win_ref, wout_ref), (win, wout), sems)
    interact_body(copies, (win, wout), moved_ref, active, updated_refs)


def first_step(moved, win, wout, row_dev):
    bins, points = moved.shape
    terms = win.shape[0]
    return pl.pallas_call(
        first_kernel,
        out_shape=[jax.ShapeDtypeStruct((bins, points // row_dev), jnp.bfloat16)] * row_dev,
        in_specs=[VMEM, ANY, ANY],
        out_specs=[VMEM] * row_dev,
        scratch_shapes=weight_scratch(win, wout, points),
        compiler_params=pltpu.CompilerParams(vmem_limit_bytes=28 * 1024 * 1024),
        cost_estimate=pl.CostEstimate(flops=4 * bins * terms * points, bytes_accessed=4 * bins * terms, transcendentals=terms * points),
        name="first_step",
    )(moved, *in_hbm(win, wout))


def second_kernel(win_ref, wout_ref, drift_ref, ocean_ref, land_ref, *refs):
    *row_refs, whole, win, wout, active, sems, moved = refs
    copies = weight_copies((win_ref, wout_ref), (win, wout), sems)
    bins, cols = row_refs[0].shape
    row_dev = len(row_refs) - 2
    size = 16
    count = bins // size

    @pl.loop(0, count, unroll=8 if count % 8 == 0 else 1)
    def _(i):
        at = pl.ds(pl.multiple_of(i * size, size), size)
        rows = [ref[at, :].astype(jnp.float32) for ref in row_refs]
        drift_x, drift_y = (wide(drift_ref, s, at, cols) for s in range(2))
        for j in range(row_dev):
            lanes = slice(j * cols, (j + 1) * cols)
            east, north = (ocean_ref[s, 0:1, lanes] for s in range(2))
            new = upwind(rows[j + 1], rows[j], rows[j + 2], drift_x, drift_y, east, north, land_ref[:, lanes])
            moved[at, lanes] = new.astype(jnp.bfloat16)

    interact_body(copies, (win, wout), moved, active, (whole,))


def second_step(rows, win, wout, drift, ocean, land):
    bins, cols = rows[0].shape
    points = cols * (len(rows) - 2)
    terms = win.shape[0]
    return pl.pallas_call(
        second_kernel,
        out_shape=jax.ShapeDtypeStruct((bins, points), jnp.bfloat16),
        in_specs=[ANY, ANY] + [VMEM] * (3 + len(rows)),
        out_specs=VMEM,
        scratch_shapes=weight_scratch(win, wout, points) + [pltpu.VMEM((bins, points), jnp.bfloat16)],
        compiler_params=pltpu.CompilerParams(vmem_limit_bytes=28 * 1024 * 1024),
        cost_estimate=pl.CostEstimate(flops=4 * bins * terms * points, bytes_accessed=4 * bins * terms, transcendentals=terms * points),
        name="second_step",
    )(*in_hbm(win, wout), drift, ocean, land, *rows)


def ocean_kernel(ocean_ref, above_ref, below_ref, stokes_ref, wind_ref, inverse_ref, land_ref, latitude_ref, *refs):
    *wave_refs, out_ref = refs
    levels, points = ocean_ref.shape[1:]
    cols = above_ref.shape[2]
    row_dev = points // cols
    turn = time_step * latitude_ref[...]
    top = lax.broadcasted_iota(jnp.int32, (levels, points), 0) == 0
    for s in range(2):
        center = ocean_ref[s]
        drift = [
            jnp.dot(stokes_ref[1 - s], ref[...], preferred_element_type=jnp.float32) for ref in wave_refs
        ]
        other = ocean_ref[1 - s] + (drift[0] if len(drift) == 1 else jnp.concatenate(drift, axis=1))
        pieces = [center[:, j * cols : (j + 1) * cols] for j in range(row_dev)]
        rows = [above_ref[s]] + pieces + [below_ref[s]]
        around = [
            rows[j] + rows[j + 2] + pltpu.roll(rows[j + 1], 1, 1) + pltpu.roll(rows[j + 1], cols - 1, 1)
            for j in range(row_dev)
        ]
        lateral = diffusion * (jnp.concatenate(around, axis=1) - 4.0 * center)
        swing = turn * other
        forced = center + (swing if s == 0 else -swing) + lateral
        forced = forced + jnp.where(top, time_step * wind_ref[s : s + 1, :], 0.0)
        mixed = jnp.dot(inverse_ref[...], forced, precision=lax.Precision.HIGHEST, preferred_element_type=jnp.float32)
        out_ref[s] = mixed * land_ref[...]


def ocean_step(ocean, above, below, stokes, wind, inverse, land, latitude, waves):
    return pl.pallas_call(
        ocean_kernel,
        out_shape=jax.ShapeDtypeStruct(ocean.shape, jnp.float32),
        in_specs=[VMEM] * (8 + len(waves)),
        out_specs=VMEM,
        compiler_params=pltpu.CompilerParams(vmem_limit_bytes=8 * 1024 * 1024),
        cost_estimate=pl.CostEstimate(flops=12 * inverse.shape[0] * ocean.size, bytes_accessed=12 * ocean.size, transcendentals=0),
        name="ocean_step",
    )(ocean, above, below, stokes, wind, inverse, land, latitude, *waves)


def gather_kernel(parts_ref, out_ref, *planes):
    devices, bins, points = parts_ref.shape
    rows, cols = out_ref.shape[1:]
    row_dev, pitch = rows // devices, rows + PAD
    size = 24 if bins % 24 == 0 else 8

    @pl.loop(0, devices)
    def _(d):
        for b in range(0, bins, size):
            part = parts_ref[d, b : b + size, :].astype(jnp.float32)
            for j in range(row_dev):
                at = pl.ds(b * pitch + d * row_dev + j, size, stride=pitch)
                for h, ref in enumerate(planes):
                    low = j * cols + h * 128
                    ref[at, :] = part[:, low : low + 128]

    @pl.loop(0, bins, unroll=8)
    def _(b):
        at = pl.ds(pl.multiple_of(b * pitch, 8), rows)
        out_ref[b] = jnp.concatenate([ref[at, :] for ref in planes], axis=1).astype(jnp.bfloat16)


def gather_rows(parts, rows, cols):
    bins = parts.shape[1]
    return pl.pallas_call(
        gather_kernel,
        out_shape=jax.ShapeDtypeStruct((bins, rows, cols), jnp.bfloat16),
        in_specs=[VMEM],
        out_specs=VMEM,
        scratch_shapes=[pltpu.VMEM((bins * (rows + PAD), 128), jnp.float32)] * (cols // 128),
        compiler_params=pltpu.CompilerParams(vmem_limit_bytes=20 * 1024 * 1024),
        cost_estimate=pl.CostEstimate(flops=parts.size, bytes_accessed=4 * parts.size, transcendentals=0),
        name="gather_rows",
    )(parts)


def shifts(size):
    up = [(i, i + 1) for i in range(size - 1)]
    return up, [(j, i) for i, j in up]


def exchange(value):
    return lax.all_to_all(value, "grid", split_axis=0, concat_axis=0, tiled=True)


def per_device(
    spectrum,
    ocean_currents,
    wind_stress,
    land_mask,
    bin_drift,
    coupling_in,
    coupling_out,
    stokes_weight,
    mixing_inverse,
):
    device = lax.axis_index("grid")
    devices = lax.axis_size("grid")
    bins, rows, cols = spectrum.shape
    row_dev = rows // devices
    levels = ocean_currents.shape[1]
    points = row_dev * cols
    up, down = shifts(devices)
    me = device.astype(jnp.int32).reshape(1)

    tops = jnp.broadcast_to(ocean_currents[:, 0][None], (devices, 2, row_dev, cols))
    tops = exchange(tops)
    ocean_above = lax.ppermute(ocean_currents[:, :, -1], "grid", up)
    ocean_below = lax.ppermute(ocean_currents[:, :, 0], "grid", down)

    stokes = stokes_weight.reshape(2, levels, -1)
    drift = jnp.broadcast_to(bin_drift[:, :, None], bin_drift.shape + (128,))
    land = lax.dynamic_slice_in_dim(land_mask, device * row_dev, row_dev, 0)
    land = land.astype(jnp.float32).reshape(1, points)
    place = (device * row_dev + jnp.arange(row_dev, dtype=jnp.int32)).astype(jnp.float32)
    latitude = jnp.sin(math.pi * ((place + 0.5) / rows - 0.5))
    latitude = jnp.broadcast_to(latitude[:, None], (row_dev, cols)).reshape(1, points)
    wind = wind_stress.reshape(2, points)
    ocean = ocean_currents.reshape(2, levels, points)

    moved = move_bins(me, spectrum, tops, land_mask, drift)
    moved, coupling_in, coupling_out = lax.optimization_barrier((moved, coupling_in, coupling_out))
    win, wout = turn_weights(*in_hbm(coupling_in, coupling_out))
    moved = exchange(moved)
    moved, win, wout, stokes, ocean_above, ocean_below, ocean, wind, land, latitude = lax.optimization_barrier(
        (moved, win, wout, stokes, ocean_above, ocean_below, ocean, wind, land, latitude)
    )
    updated = first_step(moved.reshape(-1, points), win, wout, row_dev)
    above = lax.ppermute(updated[-1], "grid", up)
    below = lax.ppermute(updated[0], "grid", down)
    ocean = ocean_step(ocean, ocean_above, ocean_below, stokes, wind, mixing_inverse, land, latitude, updated)
    whole = second_step([above, *updated, below], win, wout, drift, ocean, land)
    spectra = exchange(whole.reshape(devices, bins, points))
    ocean_above = lax.ppermute(ocean[:, :, -cols:], "grid", up)
    ocean_below = lax.ppermute(ocean[:, :, :cols], "grid", down)
    ocean = ocean_step(ocean, ocean_above, ocean_below, stokes, wind, mixing_inverse, land, latitude, [whole])
    return gather_rows(spectra, rows, cols), ocean.reshape(2, levels, row_dev, cols)


def padded_2(value, sides, width):
    for axis, dim in sides:
        size, length = (lax.axis_size(axis), value.shape[dim])
        up = [(i, (i + 1) % size) for i in range(size - 1)]
        down = [(j, i) for i, j in up]
        last = lax.slice_in_dim(value, length - width, length, axis=dim)
        first = lax.slice_in_dim(value, 0, width, axis=dim)
        before = lax.ppermute(last, axis, up)
        after = lax.ppermute(first, axis, down)
        value = jnp.concatenate([before, value, after], axis=dim)
    return value


def plain_advect(center, above, below, east_flow, north_flow, drift, land):
    speed_x = reach * jnp.tanh(drift[0][:, None, None] + east_flow[None])
    speed_y = reach * jnp.tanh(drift[1][:, None, None] + north_flow[None])
    western = jnp.roll(center, 1, axis=2)
    eastern = jnp.roll(center, -1, axis=2)
    change = jnp.maximum(speed_x, 0.0) * (center - western) + jnp.minimum(speed_x, 0.0) * (
        eastern - center
    )
    change = (
        change
        + jnp.maximum(speed_y, 0.0) * (center - above)
        + jnp.minimum(speed_y, 0.0) * (below - center)
    )
    return (center - change) * land[None]


def plain_interact(points, coupling_in, coupling_out, stokes_weight):
    bins, rows, cols = points.shape
    flat = points.reshape(bins, rows * cols)
    terms = lax.dot_general(
        flat, coupling_in, (((0,), (0,)), ((), ())), preferred_element_type=jnp.float32
    )
    active = (terms * jnp.tanh(terms)).astype(jnp.bfloat16)
    source = lax.dot_general(
        coupling_out, active, (((0,), (1,)), ((), ())), preferred_element_type=jnp.float32
    )
    updated = (flat.astype(jnp.float32) + source).astype(jnp.bfloat16)
    profile = jnp.dot(stokes_weight, updated, preferred_element_type=jnp.float32)
    return (updated.reshape(bins, rows, cols), profile.reshape(2, -1, rows, cols))


def plain_ocean_update(padded, stokes, wind, inverse, land, latitude):
    center = padded[:, :, 1:-1]
    lateral = diffusion * (
        padded[:, :, :-2]
        + padded[:, :, 2:]
        + jnp.roll(center, 1, axis=3)
        + jnp.roll(center, -1, axis=3)
        - 4.0 * center
    )
    coriolis = latitude[None, :, None]
    eastward = center[0] + time_step * coriolis * (center[1] + stokes[1]) + lateral[0]
    northward = center[1] - time_step * coriolis * (center[0] + stokes[0]) + lateral[1]
    eastward = eastward.at[0].add(time_step * wind[0])
    northward = northward.at[0].add(time_step * wind[1])
    forced = jnp.stack([eastward, northward])
    mixed = jnp.einsum("kl,slrc->skrc", inverse, forced, precision=lax.Precision.HIGHEST)
    return mixed * land[None, None]


def plain_device(
    spectrum,
    ocean_currents,
    wind_stress,
    land_mask,
    bin_drift,
    coupling_in,
    coupling_out,
    stokes_weight,
    mixing_inverse,
):
    device = lax.axis_index("grid")
    device_count = lax.axis_size("grid")
    rows_dev = ocean_currents.shape[2]
    total_rows = rows_dev * device_count
    land = land_mask.astype(jnp.float32)
    land_local = lax.dynamic_slice_in_dim(land, device * rows_dev, rows_dev, 0)
    row_place = (device * rows_dev + jnp.arange(rows_dev, dtype=jnp.int32)).astype(jnp.float32)
    latitude = jnp.sin(math.pi * ((row_place + 0.5) / total_rows - 0.5))
    ocean = ocean_currents
    points = lax.all_to_all(spectrum, "grid", split_axis=1, concat_axis=0, tiled=True)
    for turn_index in range(STEPS):
        padded = padded_2(points, (("grid", 1),), 1).astype(jnp.float32)
        moved = plain_advect(
            padded[:, 1:-1],
            padded[:, :-2],
            padded[:, 2:],
            ocean[0, 0],
            ocean[1, 0],
            bin_drift,
            land_local,
        ).astype(jnp.bfloat16)
        updated, stokes = plain_interact(moved, coupling_in, coupling_out, stokes_weight)
        ocean_padded = padded_2(ocean, (("grid", 2),), 1)
        points = updated
        ocean = plain_ocean_update(
            ocean_padded, stokes, wind_stress, mixing_inverse, land_local, latitude
        )
    spectra = lax.all_to_all(points, "grid", split_axis=0, concat_axis=1, tiled=True)
    return (spectra, ocean)


def solution(mesh):
    def body(spectrum, *others):
        aligned = spectrum.shape[0] % 8 == 0 and spectrum.shape[2] % 128 == 0
        return (per_device if aligned else plain_device)(spectrum, *others)

    return jax.shard_map(
        body,
        mesh=mesh,
        in_specs=(
            P("grid", "member", None),
            P(None, None, ("member", "grid"), None),
            P(None, ("member", "grid"), None),
            P(),
            P(),
            P(),
            P(),
            P(),
            P(),
        ),
        out_specs=(P("grid", "member", None), P(None, None, ("member", "grid"), None)),
        check_vma=False,
    )
```
